512 devices in a mesh: dp: 8 (over z_lo, core), ctx: 64 (over y, x, z_hi).
Axes of the slice: x: 4, y: 8, z: 8 (z_hi: 2, z_lo: 4; z = z_hi * 4 + z_lo), core: 2. Of those that a mesh axis runs over, the one named last changes fastest.
Arguments:
- queries: bfloat16 [65536, 1024], P(('dp', 'ctx')), parts along dimension 0, may hold values from -6 to 6
- keys: bfloat16 [65536, 256], P(('dp', 'ctx')), parts along dimension 0, may hold values from -6 to 6
- values: bfloat16 [65536, 256], P(('dp', 'ctx')), parts along dimension 0, may hold values from -6 to 6
- positions: int32 [65536], P(('dp', 'ctx')), parts along dimension 0, may hold values from 0 to 8191, as said below
Outputs:
- attended: bfloat16 [65536, 1024], P(('dp', 'ctx')), parts along dimension 0
- log_sum_exp: float32 [8, 65536], P(None, ('dp', 'ctx')), parts along dimension 1
The draws below stay inside these ranges and needn't reach their ends.
There are 8 independent parts, one for each index of `dp`. The reference program is written for one: setup_inputs(seed, part) draws one part's arguments, and reference() takes and returns one part's arrays. A program takes and returns all parts, laid end to end along the dimension named above; each array names one. Nothing has to cross between parts.
Inputs may be any that keep to these rules, and one draw needn't show every extreme that they name: A permutation of the positions of one book; each index of ctx holds two runs of 64 consecutive positions, first run number c, then run number 2 * 64 - 1 - c, in units of 64 positions.
All inputs are finite; a program needn't handle non-finite values.
Results may differ from the reference program's by a relative error of at most 0.0055.
Values may be sent and summed in bfloat16 or wider, within the bound.
A program may use at most 64 MiB of HBM per device.

```python
import math
import jax
import jax.numpy as jnp
from jax import lax

HD = 128
QH = 8
KVH = 2
TOK_DEV = 128
SEQ = 8192


def paired_positions(key):
    devices = SEQ // TOK_DEV
    order = jax.random.permutation(jax.random.fold_in(key, 11), devices)
    rows = jnp.arange(SEQ, dtype=jnp.int32)
    device = rows // TOK_DEV
    within = rows % TOK_DEV
    half = TOK_DEV // 2
    first = order[device]
    block = jnp.where(within < half, first, 2 * devices - 1 - first)
    return (block * half + within % half).astype(jnp.int32)


def draw_positions(key, part):
    return paired_positions(key)


def draw_queries(key, part):
    base = jnp.clip(jax.random.normal(jax.random.fold_in(key, 21), (SEQ, QH * HD), jnp.float32) * 1.7, -6.0, 6.0)
    return base.astype(jnp.bfloat16)


def draw_keys(key, part):
    base = jnp.clip(jax.random.normal(jax.random.fold_in(key, 22), (SEQ, KVH * HD), jnp.float32) * 1.7, -6.0, 6.0)
    return base.astype(jnp.bfloat16)


def block_levels(own_key, shape, split, low, largest):
    level, own = 1.0, jax.random.fold_in(own_key, 6)
    for position, shards_of in split:
        heights = jnp.exp(jax.random.uniform(jax.random.fold_in(own, position), (shards_of,), jnp.float32, low / len(split), largest / len(split)))
        level = level * jnp.repeat(heights, shape[position] // shards_of).reshape([-1 if axis == position else 1 for axis in range(len(shape))])
    return level


def gaussian(own_key, shape, scale, limit, split=(), held_as=jnp.bfloat16):
    values = scale * jax.random.normal(own_key, shape, jnp.float32)
    if split:
        values = values * block_levels(own_key, shape, split, -0.22, 0.18)
    return jnp.clip(values, -limit, limit).astype(held_as)


def setup_inputs(seed: int = 0, part: int = 0) -> dict:
    seeds = jax.random.split(jax.random.key(seed), 5)
    part_keys = jax.random.split(jax.random.fold_in(seeds[4], part), 5)
    return {
        "queries": draw_queries(jax.random.fold_in(jax.random.fold_in(seeds[4], part), 71), part),
        "keys": draw_keys(jax.random.fold_in(jax.random.fold_in(seeds[4], part), 71), part),
        "values": gaussian(part_keys[2], (SEQ, KVH * HD), 1.0, 6.0, ((0, 64),)),
        "positions": draw_positions(jax.random.fold_in(jax.random.fold_in(seeds[4], part), 71), part),
    }


def reference(queries, keys, values, positions):
    total_rows = queries.shape[0]
    groups = QH // KVH
    block_rows = math.gcd(total_rows, 512)
    key_heads = keys.reshape(total_rows, KVH, HD).astype(jnp.float32)
    value_heads = values.reshape(total_rows, KVH, HD).astype(jnp.float32)
    query_heads = queries.reshape(total_rows, KVH, groups, HD)

    def one_block(index):
        start = (index * block_rows).astype(jnp.int32)
        block_q = lax.dynamic_slice_in_dim(query_heads, start, block_rows, 0).astype(jnp.float32)
        block_pos = lax.dynamic_slice_in_dim(positions, start, block_rows, 0)
        scores = jnp.einsum("qhgd,khd->hgqk", block_q, key_heads) * (HD ** -0.5)
        allowed = block_pos[:, None] >= positions[None, :]
        scores = jnp.where(allowed, scores, -1e30)
        peak = jnp.max(scores, axis=-1)
        weights = jnp.where(allowed, jnp.exp(scores - peak[..., None]), 0.0)
        denominators = jnp.sum(weights, axis=-1)
        rounded = lax.optimization_barrier(weights.astype(jnp.bfloat16)).astype(jnp.float32)
        summed = jnp.einsum("hgqk,khd->hgqd", rounded, value_heads)
        output = summed / denominators[..., None]
        output = jnp.transpose(output, (2, 0, 1, 3)).reshape(block_rows, QH * HD).astype(jnp.bfloat16)
        log_total = (peak + jnp.log(denominators)).reshape(QH, block_rows)
        return output, log_total

    outputs, log_totals = lax.map(one_block, jnp.arange(total_rows // block_rows, dtype=jnp.int32))
    attended = outputs.reshape(total_rows, QH * HD)
    log_sum_exp = jnp.transpose(log_totals, (1, 0, 2)).reshape(QH, total_rows)
    return attended, log_sum_exp
```

```python
import functools
import math

import jax
import jax.numpy as jnp
from jax import lax
from jax.experimental import pallas as pl
from jax.experimental.pallas import tpu as pltpu
from jax.sharding import PartitionSpec as P

MESH = pl.DeviceIdType.MESH
F32 = jnp.float32
BF16 = jnp.bfloat16
HD = 128
QH = 8
KVH = 2
GROUP = QH // KVH
TOK = 128
RUN = 64
NX, NY, NZ = 4, 8, 2
SCALE = math.log2(math.e) / math.sqrt(HD)
NEG = -1e30
KV_ROWS = 4 * RUN
Q_ROWS = 2 * GROUP * RUN
META = 16
OWN, Z0 = 0, 1
OM = {0: OWN, 1: 2, 2: 4, 3: 8, 4: 12}
OP = {0: OWN, 1: 3, 2: 5, 3: 9, 4: 12}
ZM = {0: Z0, 1: 6, 2: 10, 3: 13, 4: 15}
ZP = {0: Z0, 1: 7, 2: 11, 3: 14, 4: 15}
SLOTS = 16
CHUNK = 4
X_STEP = {1: 1, 2: NX - 1, 3: 2}
X_BACK = {1: 2, 2: 1, 3: 3}


def nt(a, b):
    return lax.dot_general(a, b, (((1,), (1,)), ((), ())), preferred_element_type=F32)


def nn(a, b):
    return lax.dot_general(a, b, (((1,), (0,)), ((), ())), preferred_element_type=F32)


def lanes(x, n):
    return jnp.concatenate([x] * (n // HD), axis=1)


def fold(q, parts, m_ref, l_ref, a_ref, first):
    scores = []
    for k, unused_v, bias in parts:
        s = nt(q, k)
        scores.append(s if bias is None else s + bias)
    peak = functools.reduce(jnp.maximum, [jnp.max(s, axis=1, keepdims=True) for s in scores])
    if first:
        new = jnp.broadcast_to(peak, m_ref.shape)
    else:
        old = m_ref[...]
        new = jnp.maximum(old, peak)
    shift = new * SCALE
    total = None
    update = None
    for s, (unused_k, v, unused_bias) in zip(scores, parts):
        p = jnp.exp2(s * SCALE - lanes(shift, s.shape[1]))
        for i in range(s.shape[1] // HD):
            piece = p[:, i * HD : (i + 1) * HD]
            total = piece if total is None else total + piece
        pv = nn(p.astype(BF16), v)
        update = pv if update is None else update + pv
    if first:
        l_ref[...] = total
        a_ref[...] = update
    else:
        shrink = jnp.exp2(old * SCALE - shift)
        l_ref[...] = l_ref[...] * shrink + total
        a_ref[...] = a_ref[...] * shrink + update
    m_ref[...] = new


def kernel(
    pos_ref, q_ref, k_ref, v_ref, out_ref, lse_ref,
    kv, qb, ob, osend, m, l, a,
    kv_send, kv_recv, q_send, q_recv, o_send, o_recv,
):
    me = lax.axis_index("ctx")
    my_y, my_x, my_z = me // (NX * NZ), lax.rem(me // NZ, NX), lax.rem(me, NZ)

    def at(dy, dx, dz):
        y, x, z = lax.rem(my_y + dy, NY), lax.rem(my_x + dx, NX), lax.rem(my_z + dz, NZ)
        return {"ctx": (y * NX + x) * NZ + z}

    up, down, across = at(1, 0, 0), at(NY - 1, 0, 0), at(0, 0, 1)
    row = {i: at(0, X_STEP[i], 0) for i in (1, 2, 3)}
    barrier = pltpu.get_barrier_semaphore()
    for peer in (across, row[3], up, down, row[1], row[2]):
        pl.semaphore_signal(barrier, inc=1, device_id=peer, device_id_type=MESH)

    number = lax.shift_right_logical(pos_ref[...], 6)
    low = jnp.minimum(number, 2 * RUN - 1 - number)
    lane = lax.broadcasted_iota(jnp.int32, (1, HD), 1)
    swapped = jnp.where((low == number) == (lane < RUN), 0.0, 1.0)
    meta = jnp.broadcast_to(low.astype(F32), (META, HD)).astype(BF16)
    turn = jnp.broadcast_to(swapped, (RUN, HD)).astype(BF16) > 0.5

    def half(ref, r, cols):
        return jnp.where(turn, ref[(1 - r) * RUN : (2 - r) * RUN, cols], ref[r * RUN : (r + 1) * RUN, cols])

    def stage_kv(h):
        cols = slice(h * HD, (h + 1) * HD)
        for r in range(2):
            kv[h, OWN, r * RUN : (r + 1) * RUN, :] = half(k_ref, r, cols)
            kv[h, OWN, (2 + r) * RUN : (3 + r) * RUN, :] = half(v_ref, r, cols)
        if h == 0:
            kv[h, OWN, KV_ROWS:, :] = meta

    def stage_q(h):
        for r in range(2):
            for g in range(GROUP):
                base = (r * GROUP + g) * RUN
                cols = slice((h * GROUP + g) * HD, (h * GROUP + g + 1) * HD)
                qb[h, 0, base : base + RUN, :] = half(q_ref, r, cols)
        if h == 0:
            qb[h, 0, Q_ROWS:, :] = meta

    started = []

    def kv_copy(h, src, dst, device):
        n = KV_ROWS + (META if h == 0 else 0)
        return pltpu.make_async_remote_copy(
            src_ref=kv.at[h, src, 0:n], dst_ref=kv.at[h, dst, 0:n],
            send_sem=kv_send.at[h, dst], recv_sem=kv_recv.at[h, dst],
            device_id=device, device_id_type=MESH,
        )

    def send_kv(h, src, dst, device):
        copy = kv_copy(h, src, dst, device)
        copy.start()
        started.append(copy)

    def got_kv(h, slot):
        kv_copy(h, slot, slot, up).wait_recv()

    def q_copy(h, i):
        n = Q_ROWS + (META if h == 0 else 0)
        return pltpu.make_async_remote_copy(
            src_ref=qb.at[h, 0, 0:n], dst_ref=qb.at[h, X_BACK[i], 0:n],
            send_sem=q_send.at[h, i], recv_sem=q_recv.at[h, X_BACK[i]],
            device_id=row[i], device_id_type=MESH,
        )

    def o_copy(h, i):
        return pltpu.make_async_remote_copy(
            src_ref=osend.at[h, i], dst_ref=ob.at[h, X_BACK[i]],
            send_sem=o_send.at[h, i], recv_sem=o_recv.at[h, X_BACK[i]],
            device_id=row[i], device_id_type=MESH,
        )

    def ring(h, step, o_part, z_part):
        if step < NY // 2 - 1:
            both = ((OM, up), (OP, down)) if o_part else ((ZM, up), (ZP, down))
            for slots, device in both:
                if step > 0:
                    got_kv(h, slots[step])
                send_kv(h, slots[step], slots[step + 1], device)
        else:
            both = (OM, OP) if o_part else (ZM, ZP)
            for slots in both:
                got_kv(h, slots[step])
            slots, device = (both[0], up) if h == 0 else (both[1], down)
            send_kv(h, slots[step], slots[step + 1], device)

    stage_kv(0)
    stage_kv(1)
    stage_q(0)
    stage_q(1)
    pl.semaphore_wait(barrier, 6)
    for h in range(KVH):
        send_kv(h, OWN, Z0, across)
        ring(h, 0, True, False)
    for h in range(KVH):
        for i in (3, 1, 2):
            q_copy(h, i).start()

    lane64 = lane < RUN
    wide = CHUNK * RUN

    def attend(h, chunk):
        first = chunk == 0
        s0 = chunk * CHUNK
        block = [kv[h, s0 : s0 + CHUNK, i * RUN : (i + 1) * RUN, :].reshape(wide, HD) for i in range(4)]
        run = [kv[0, s0 + i, KV_ROWS : KV_ROWS + META, :].astype(F32)[0:1] for i in range(CHUNK)]
        theirs = jnp.concatenate(
            [jnp.where(lane64, run[i], run[i + 1]) for i in range(0, CHUNK, 2)], axis=1
        )
        for c in range(NX):
            mine = lanes(qb[0, c, Q_ROWS : Q_ROWS + META, :].astype(F32)[0:1], wide)
            bias1 = jnp.where(theirs < mine, 0.0, NEG)
            bias2 = jnp.where(theirs > mine, 0.0, NEG)
            if first and c == 0:
                token = lax.rem(lax.broadcasted_iota(jnp.int32, (GROUP * RUN, wide), 0), RUN)
                column = lax.broadcasted_iota(jnp.int32, (GROUP * RUN, wide), 1)
                bias1 = jnp.where(column <= token, 0.0, bias1)
                bias2 = jnp.where(column <= token, 0.0, bias2)
            q1 = qb[h, c, 0 : GROUP * RUN, :]
            q2 = qb[h, c, GROUP * RUN : Q_ROWS, :]
            k1, k2, v1, v2 = block
            fold(q2, [(k1, v1, None), (k2, v2, bias2)], m.at[h, c, 1], l.at[h, c, 1], a.at[h, c, 1], first)
            fold(q1, [(k1, v1, bias1)], m.at[h, c, 0], l.at[h, c, 0], a.at[h, c, 0], first)

    eye = lax.broadcasted_iota(jnp.int32, (HD, HD), 0) == lax.broadcasted_iota(jnp.int32, (HD, HD), 1)

    def close(h, c, dst):
        logs = []
        for r in range(2):
            total = jnp.sum(l[h, c, r], axis=1, keepdims=True)
            dst[r * GROUP * RUN : (r + 1) * GROUP * RUN, :] = (a[h, c, r] * (1.0 / total)).astype(BF16)
            logs.append(m[h, c, r] * SCALE + jnp.log2(total))
        rows = []
        for g in range(GROUP):
            both = jnp.concatenate([logs[r][g * RUN : (g + 1) * RUN] for r in range(2)], axis=0)
            rows.append(jnp.sum(jnp.where(eye, both, 0.0), axis=0, keepdims=True))
        rest = jnp.concatenate(rows, axis=0)
        pieces = []
        for unused in range(3):
            piece = rest.astype(BF16).astype(F32)
            rest = rest - piece
            pieces.append(piece)
        pieces.append(jnp.zeros_like(rest))
        dst[Q_ROWS:, :] = jnp.concatenate(pieces, axis=0).astype(BF16)

    def finish(h):
        for i in (3, 1, 2):
            close(h, i, osend.at[h, i])
            o_copy(h, i).start()
        close(h, 0, ob.at[h, 0])

    to_row = lax.broadcasted_iota(jnp.int32, (HD, HD), 0)
    from_row = lax.broadcasted_iota(jnp.int32, (HD, HD), 1)
    place = to_row == jnp.where(swapped > 0.5, lax.bitwise_xor(from_row, RUN), from_row)

    def merge(h):
        for i in (1, 2, 3):
            o_copy(h, i).wait_recv()
        logs = []
        for i in range(NX):
            t = ob[h, i, Q_ROWS:, :].astype(F32)
            logs.append(t[0:4] + t[4:8] + t[8:12])
        top = functools.reduce(jnp.maximum, logs)
        weights = [jnp.exp2(x - top) for x in logs]
        total = sum(weights[1:], weights[0])
        whole = (top + jnp.log2(total)) * math.log(2.0)
        turned = jnp.concatenate([whole[:, RUN:], whole[:, :RUN]], axis=1)
        lse_ref[h * GROUP : (h + 1) * GROUP, :] = jnp.where(swapped > 0.5, turned, whole)
        weights = [w / total for w in weights]
        for g in range(GROUP):
            left, right = [], []
            for i in range(NX):
                diagonal = jnp.where(place, weights[i][g : g + 1, :], 0.0)
                high = diagonal.astype(BF16)
                left += [high, (diagonal - high.astype(F32)).astype(BF16)]
                part = [ob[h, i, (r * GROUP + g) * RUN : (r * GROUP + g + 1) * RUN, :] for r in range(2)]
                right += part + part
            o = nn(jnp.concatenate(left, axis=1), jnp.concatenate(right, axis=0))
            cols = slice((h * GROUP + g) * HD, (h * GROUP + g + 1) * HD)
            out_ref[:, cols] = o.astype(BF16)

    def got_q(h):
        for i in (1, 2, 3):
            q_copy(h, i).wait_recv()

    for h in range(KVH):
        ring(h, 1, True, False)
    for h in range(KVH):
        got_kv(h, Z0)
        ring(h, 0, False, True)
    got_q(0)
    attend(0, 0)
    for h in range(KVH):
        ring(h, 2, True, False)
    for h in range(KVH):
        ring(h, 1, False, True)
    got_q(1)
    attend(1, 0)
    attend(0, 1)
    for h in range(KVH):
        ring(h, 3, True, False)
    for h in range(KVH):
        ring(h, 2, False, True)
    attend(1, 1)
    attend(0, 2)
    for h in range(KVH):
        got_kv(h, OM[4])
    for h in range(KVH):
        ring(h, 3, False, True)
    attend(1, 2)
    for h in range(KVH):
        got_kv(h, ZM[4])
        attend(h, 3)
        finish(h)
    for h in range(KVH):
        merge(h)
    for copy in started:
        copy.wait_send()
    for h in range(KVH):
        for i in (1, 2, 3):
            q_copy(h, i).wait_send()
            o_copy(h, i).wait_send()


def shards(queries, keys, values, positions):
    vmem = pl.BlockSpec(memory_space=pltpu.VMEM)
    state = (KVH, NX, 2, GROUP * RUN, HD)
    return pl.pallas_call(
        kernel,
        name="ring_attention",
        out_shape=(
            jax.ShapeDtypeStruct((TOK, QH * HD), BF16),
            jax.ShapeDtypeStruct((QH, TOK), F32),
        ),
        in_specs=[vmem, vmem, vmem, vmem],
        out_specs=(vmem, vmem),
        scratch_shapes=[
            pltpu.VMEM((KVH, SLOTS, KV_ROWS + META, HD), BF16),
            pltpu.VMEM((KVH, NX, Q_ROWS + META, HD), BF16),
            pltpu.VMEM((KVH, NX, Q_ROWS + META, HD), BF16),
            pltpu.VMEM((KVH, NX, Q_ROWS + META, HD), BF16),
            pltpu.VMEM(state, F32),
            pltpu.VMEM(state, F32),
            pltpu.VMEM(state, F32),
            pltpu.SemaphoreType.DMA((KVH, SLOTS)),
            pltpu.SemaphoreType.DMA((KVH, SLOTS)),
            pltpu.SemaphoreType.DMA((KVH, NX)),
            pltpu.SemaphoreType.DMA((KVH, NX)),
            pltpu.SemaphoreType.DMA((KVH, NX)),
            pltpu.SemaphoreType.DMA((KVH, NX)),
        ],
        compiler_params=pltpu.CompilerParams(
            collective_id=0, has_side_effects=True, vmem_limit_bytes=40 * 2**20
        ),
    )(positions.reshape(1, TOK), queries, keys, values)


def solution(mesh):
    return jax.shard_map(
        shards,
        mesh=mesh,
        in_specs=(
            P(("dp", "ctx"), None),
            P(("dp", "ctx"), None),
            P(("dp", "ctx"), None),
            P(("dp", "ctx")),
        ),
        out_specs=(P(("dp", "ctx"), None), P(None, ("dp", "ctx"))),
        check_vma=False,
    )
```

```python
import functools
import math

import jax
import jax.numpy as jnp
from jax import lax
from jax.experimental import pallas as pl
from jax.experimental.pallas import tpu as pltpu
from jax.sharding import PartitionSpec as P

MESH = pl.DeviceIdType.MESH
F32 = jnp.float32
BF16 = jnp.bfloat16
HD = 128
QH = 8
KVH = 2
GROUP = QH // KVH
TOK = 128
RUN = 64
NX, NY, NZ = 4, 8, 2
SCALE = math.log2(math.e) / math.sqrt(HD)
NEG = -1e6
KV_ROWS = 4 * RUN
Q_ROWS = 2 * GROUP * RUN
META = 16
CHUNKS = (
    (("OO", 0), ("OX", 0), ("OO", -1), ("OO", 1)),
    (("OX", -1), ("OX", 1), ("OO", -2), ("OO", 2)),
    (("OX", -2), ("OX", 2), ("ZO", 0), ("ZX", 0)),
    (("OO", -3), ("OO", 3), ("OX", -3), ("OX", 3)),
    (("ZO", -1), ("ZO", 1), ("ZX", -1), ("ZX", 1)),
    (("OO", 4), ("OX", 4), ("ZO", -2), ("ZO", 2)),
    (("ZX", -2), ("ZX", 2)),
    (("ZO", -3), ("ZO", 3), ("ZX", -3), ("ZX", 3)),
    (("ZO", 4), ("ZX", 4)),
)
FIRST = [sum(len(chunk) for chunk in CHUNKS[:i]) for i in range(len(CHUNKS))]
SLOT = {name: i for i, name in enumerate(name for chunk in CHUNKS for name in chunk)}
PLAN = (
    ("pass", "OO", 1), ("pass", "OX", 1),
    ("pass", "OO", 2), ("pass", "OX", 2),
    ("pass", "ZO", 0), ("pass", "ZX", 0), ("query",), ("wait", "OX", 0), ("attend", 0), ("attend", 1),
    ("pass", "OO", 3), ("pass", "OX", 3),
    ("pass", "ZO", 1), ("pass", "ZX", 1), ("attend", 2),
    ("far", "OO"), ("far", "OX"), ("attend", 3),
    ("pass", "ZO", 2), ("pass", "ZX", 2), ("attend", 4), ("attend", 5), ("attend", 6),
    ("wait", "ZO", 3), ("wait", "ZX", 3), ("attend", 7), ("wait", "ZO", 4), ("wait", "ZX", 4), ("attend", 8),
)
X_STEP = {1: 1, 2: NX - 1, 3: 2}
X_BACK = {1: 2, 2: 1, 3: 3}


def nt(a, b):
    return lax.dot_general(a, b, (((1,), (1,)), ((), ())), preferred_element_type=F32)


def nn(a, b):
    return lax.dot_general(a, b, (((1,), (0,)), ((), ())), preferred_element_type=F32)


def lanes(x, n):
    return jnp.concatenate([x] * (n // HD), axis=1)


def fold(q, k, v, bias, m_ref, l_ref, a_ref, first):
    s = nt(q, k)
    if bias.shape[0] == 1:
        bias = jnp.broadcast_to(bias, (GROUP * RUN, bias.shape[1]))
    masked = s[: GROUP * RUN] + bias
    s = masked if s.shape[0] == GROUP * RUN else jnp.concatenate([masked, s[GROUP * RUN :]], axis=0)
    peak = jnp.max(s, axis=1, keepdims=True)
    if first:
        new = jnp.broadcast_to(peak, m_ref.shape)
    else:
        old = m_ref[...]
        new = jnp.maximum(old, peak)
    shift = new * SCALE
    p = jnp.exp2(s * SCALE - lanes(shift, s.shape[1]))
    total = sum((p[:, i : i + HD] for i in range(HD, s.shape[1], HD)), p[:, :HD])
    update = nn(p.astype(BF16), v)
    if first:
        l_ref[...] = total
        a_ref[...] = update
    else:
        shrink = jnp.exp2(old * SCALE - shift)
        l_ref[...] = l_ref[...] * shrink + total
        a_ref[...] = a_ref[...] * shrink + update
    m_ref[...] = new


def kernel(
    pos_ref, q_hbm, k_hbm, v_hbm, out_ref, lse_ref,
    q_ref, k_ref, v_ref, kv, spare, qb, qspare, ob, osend, m, l, a,
    load_sem, kv_send, kv_recv, q_send, q_recv, o_send, o_recv,
):
    loads = [
        pltpu.make_async_copy(src, dst, load_sem.at[i])
        for i, (src, dst) in enumerate(((k_hbm, k_ref), (v_hbm, v_ref), (q_hbm, q_ref)))
    ]
    for load in loads:
        load.start()
    me = lax.axis_index("ctx")
    my_y, my_x, my_z = me // (NX * NZ), lax.rem(me // NZ, NX), lax.rem(me, NZ)
    head = lax.rem(my_x, 2)
    pair_step = 1 + head * (NX - 2)

    def at(dy, dx, dz):
        y, x, z = lax.rem(my_y + dy, NY), lax.rem(my_x + dx, NX), lax.rem(my_z + dz, NZ)
        return {"ctx": (y * NX + x) * NZ + z}

    up, down, across = at(1, 0, 0), at(NY - 1, 0, 0), at(0, 0, 1)
    beside, diagonal = at(0, pair_step, 0), at(0, pair_step, 1)
    above, below = at(1, pair_step, 0), at(NY - 1, pair_step, 0)
    row = {i: at(0, X_STEP[i], 0) for i in (1, 2, 3)}
    barrier = pltpu.get_barrier_semaphore()
    greet = (diagonal, across, row[3], above, below, up, down, row[1], row[2])
    for peer in greet:
        pl.semaphore_signal(barrier, inc=1, device_id=peer, device_id_type=MESH)

    number = lax.shift_right_logical(pos_ref[...], 6)
    low = jnp.minimum(number, 2 * RUN - 1 - number)
    lane = lax.broadcasted_iota(jnp.int32, (1, HD), 1)
    swapped = jnp.where((low == number) == (lane < RUN), 0.0, 1.0)
    meta = jnp.broadcast_to(low.astype(F32), (META, HD)).astype(BF16)
    turn = jnp.broadcast_to(swapped, (RUN, HD)).astype(BF16) > 0.5

    def columns(h, g, heads):
        return pl.ds(pl.multiple_of((h * heads + g) * HD, HD), HD)

    def half(ref, r, cols):
        return jnp.where(turn, ref[(1 - r) * RUN : (2 - r) * RUN, cols], ref[r * RUN : (r + 1) * RUN, cols])

    def stage_kv(h, dst):
        cols = columns(h, 0, 1)
        for r in range(2):
            dst[r * RUN : (r + 1) * RUN, :] = half(k_ref, r, cols)
            dst[(2 + r) * RUN : (3 + r) * RUN, :] = half(v_ref, r, cols)
        dst[KV_ROWS:, :] = meta

    def stage_q(h, dst):
        for r in range(2):
            for g in range(GROUP):
                base = (r * GROUP + g) * RUN
                dst[base : base + RUN, :] = half(q_ref, r, columns(h, g, GROUP))
        dst[Q_ROWS:, :] = meta

    started = []

    def kv_copy(src, slot, device):
        return pltpu.make_async_remote_copy(
            src_ref=src, dst_ref=kv.at[slot], send_sem=kv_send.at[slot], recv_sem=kv_recv.at[slot],
            device_id=device, device_id_type=MESH,
        )

    def send_kv(src, name, device):
        copy = kv_copy(src, SLOT[name], device)
        copy.start()
        started.append(copy)

    def got_kv(*name):
        if name != ("OO", 0):
            kv_copy(kv.at[SLOT[name]], SLOT[name], up).wait_recv()

    def pass_on(stream, step):
        for y, device in ((-step, up), (step, down)):
            if step or device is up:
                got_kv(stream, y)
            after = y - 1 if device is up else y + 1
            block = kv.at[SLOT[stream, y]]
            if step < 3:
                send_kv(block, (stream, after), device)
            elif stream == ("OO" if device is up else "OX"):
                send_kv(block, (stream, 4), device)

    def far(stream):
        got_kv(stream, 4)
        send_kv(kv.at[SLOT[stream, 4]], ("Z" + stream[1], 4), across)

    def wait(stream, step):
        for y in (-step, step) if 0 < step < 4 else (step,):
            got_kv(stream, y)

    def q_copy(i):
        return pltpu.make_async_remote_copy(
            src_ref=qb.at[0] if i == 3 else qspare, dst_ref=qb.at[X_BACK[i]],
            send_sem=q_send.at[i], recv_sem=q_recv.at[X_BACK[i]],
            device_id=row[i], device_id_type=MESH,
        )

    def o_copy(i):
        return pltpu.make_async_remote_copy(
            src_ref=osend.at[i], dst_ref=ob.at[X_BACK[i]],
            send_sem=o_send.at[i], recv_sem=o_recv.at[X_BACK[i]],
            device_id=row[i], device_id_type=MESH,
        )

    lane64 = lane < RUN

    def attend(chunk):
        first = chunk == 0
        s0, size = FIRST[chunk], len(CHUNKS[chunk])
        wide = size * RUN
        k1, k2, v1, v2 = [
            kv[s0 : s0 + size, i * RUN : (i + 1) * RUN, :].reshape(wide, HD) for i in range(4)
        ]
        run = [kv[s0 + i, KV_ROWS:, :].astype(F32)[0:1] for i in range(size)]
        theirs = jnp.concatenate(
            [jnp.where(lane64, run[i], run[i + 1]) for i in range(0, size, 2)], axis=1
        )
        token = lax.rem(lax.broadcasted_iota(jnp.int32, (GROUP * RUN, wide), 0), RUN)
        column = lax.rem(lax.broadcasted_iota(jnp.int32, (GROUP * RUN, wide), 1), RUN)
        triangle = jnp.where(column <= token, 0.0, NEG)
        for c in range(NX):
            mine = lanes(qb[c, Q_ROWS:, :].astype(F32)[0:1], wide)
            bias1 = jnp.where(theirs < mine, 0.0, NEG)
            bias2 = jnp.where(theirs > mine, 0.0, NEG)
            if first and c < 3:
                bias1 = jnp.where(theirs == mine, triangle, bias1)
                bias2 = jnp.where(theirs == mine, triangle, bias2)
            second = slice(GROUP * RUN, Q_ROWS)
            fold(qb[c, :Q_ROWS, :], k1, v1, bias1, m.at[c], l.at[c], a.at[c], first)
            fold(qb[c, second, :], k2, v2, bias2, m.at[c, second], l.at[c, second], a.at[c, second], False)

    eye = lax.broadcasted_iota(jnp.int32, (HD, HD), 0) == lax.broadcasted_iota(jnp.int32, (HD, HD), 1)

    def close(c, dst):
        total = jnp.sum(l[c], axis=1, keepdims=True)
        dst[:Q_ROWS, :] = (a[c] * (1.0 / total)).astype(BF16)
        logs = m[c] * SCALE + jnp.log2(total)
        rows = []
        for g in range(GROUP):
            starts = [(r * GROUP + g) * RUN for r in range(2)]
            both = jnp.concatenate([logs[i : i + RUN] for i in starts], axis=0)
            rows.append(jnp.sum(jnp.where(eye, both, 0.0), axis=0, keepdims=True))
        rest = jnp.concatenate(rows, axis=0)
        pieces = []
        for unused in range(3):
            piece = rest.astype(BF16).astype(F32)
            rest = rest - piece
            pieces.append(piece)
        pieces.append(jnp.zeros_like(rest))
        dst[Q_ROWS:, :] = jnp.concatenate(pieces, axis=0).astype(BF16)

    to_row = lax.broadcasted_iota(jnp.int32, (HD, HD), 0)
    from_row = lax.broadcasted_iota(jnp.int32, (HD, HD), 1)
    place = to_row == jnp.where(swapped > 0.5, lax.bitwise_xor(from_row, RUN), from_row)

    def merge(h, sources):
        logs = []
        for i in sources:
            t = ob[i, Q_ROWS:, :].astype(F32)
            logs.append(t[0:4] + t[4:8] + t[8:12])
        top = functools.reduce(jnp.maximum, logs)
        weights = [jnp.exp2(x - top) for x in logs]
        total = sum(weights[1:], weights[0])
        weights = [w / total for w in weights]
        for g in range(GROUP):
            left, right = [], []
            for w, i in zip(weights, sources):
                spread = jnp.where(place, w[g : g + 1, :], 0.0)
                high = spread.astype(BF16)
                left += [high, (spread - high.astype(F32)).astype(BF16)]
                part = [ob[i, (r * GROUP + g) * RUN : (r * GROUP + g + 1) * RUN, :] for r in range(2)]
                right += part + part
            o = nn(jnp.concatenate(left, axis=1), jnp.concatenate(right, axis=0))
            out_ref[:, columns(h, g, GROUP)] = o.astype(BF16)
        whole = (top + jnp.log2(total)) * math.log(2.0)
        turned = jnp.concatenate([whole[:, RUN:], whole[:, :RUN]], axis=1)
        return jnp.where(swapped > 0.5, turned, whole)

    own = kv.at[SLOT["OO", 0]]
    loads[0].wait()
    loads[1].wait()
    stage_kv(head, own)
    stage_kv(1 - head, spare)
    loads[2].wait()
    stage_q(1 - head, qspare)
    stage_q(head, qb.at[0])
    pl.semaphore_wait(barrier, len(greet))
    send_kv(own, ("ZO", 0), across)
    send_kv(spare, ("ZX", 0), diagonal)
    send_kv(own, ("OO", -1), up)
    send_kv(own, ("OO", 1), down)
    send_kv(spare, ("OX", 0), beside)
    send_kv(spare, ("OX", -1), above)
    send_kv(spare, ("OX", 1), below)
    for i in (3, 1, 2):
        q_copy(i).start()
    for what, *rest in PLAN:
        if what == "query":
            for i in (1, 2, 3):
                q_copy(i).wait_recv()
        else:
            {"pass": pass_on, "far": far, "wait": wait, "attend": attend}[what](*rest)
    for i in (3, 1, 2):
        close(i, osend.at[i])
        o_copy(i).start()
    close(0, ob.at[0])
    o_copy(3).wait_recv()
    mine = merge(head, (0, 3))
    o_copy(1).wait_recv()
    o_copy(2).wait_recv()
    other = merge(1 - head, (1, 2))
    even = jnp.where(head == 0, 1.0, 0.0)
    lse_ref[0:GROUP, :] = jnp.where(even > 0.5, mine, other)
    lse_ref[GROUP:, :] = jnp.where(even > 0.5, other, mine)
    for copy in started:
        copy.wait_send()
    for i in (1, 2, 3):
        q_copy(i).wait_send()
        o_copy(i).wait_send()


def shards(queries, keys, values, positions):
    vmem = pl.BlockSpec(memory_space=pltpu.VMEM)
    hbm = pl.BlockSpec(memory_space=pltpu.HBM)
    state = pltpu.VMEM((NX, Q_ROWS, HD), F32)
    shared = pltpu.VMEM((NX, Q_ROWS + META, HD), BF16)
    blocks = len(SLOT)
    return pl.pallas_call(
        kernel,
        name="ring_attention",
        out_shape=(
            jax.ShapeDtypeStruct((TOK, QH * HD), BF16),
            jax.ShapeDtypeStruct((QH, TOK), F32),
        ),
        in_specs=[vmem, hbm, hbm, hbm],
        out_specs=(vmem, vmem),
        scratch_shapes=[
            pltpu.VMEM((TOK, QH * HD), BF16),
            pltpu.VMEM((TOK, KVH * HD), BF16),
            pltpu.VMEM((TOK, KVH * HD), BF16),
            pltpu.VMEM((blocks, KV_ROWS + META, HD), BF16),
            pltpu.VMEM((KV_ROWS + META, HD), BF16),
            shared,
            pltpu.VMEM((Q_ROWS + META, HD), BF16),
            shared,
            shared,
            state,
            state,
            state,
            pltpu.SemaphoreType.DMA((3,)),
            pltpu.SemaphoreType.DMA((blocks,)),
            pltpu.SemaphoreType.DMA((blocks,)),
            pltpu.SemaphoreType.DMA((NX,)),
            pltpu.SemaphoreType.DMA((NX,)),
            pltpu.SemaphoreType.DMA((NX,)),
            pltpu.SemaphoreType.DMA((NX,)),
        ],
        compiler_params=pltpu.CompilerParams(
            collective_id=0, has_side_effects=True, vmem_limit_bytes=40 * 2**20
        ),
    )(positions.reshape(1, TOK), queries, keys, values)


def solution(mesh):
    return jax.shard_map(
        shards,
        mesh=mesh,
        in_specs=(
            P(("dp", "ctx"), None),
            P(("dp", "ctx"), None),
            P(("dp", "ctx"), None),
            P(("dp", "ctx")),
        ),
        out_specs=(P(("dp", "ctx"), None), P(None, ("dp", "ctx"))),
        check_vma=False,
    )
```

```python
import functools
import math

import jax
import jax.numpy as jnp
from jax import lax
from jax.experimental import pallas as pl
from jax.experimental.pallas import tpu as pltpu
from jax.sharding import PartitionSpec as P

MESH = pl.DeviceIdType.MESH
F32 = jnp.float32
BF16 = jnp.bfloat16
HD = 128
QH = 8
KVH = 2
GROUP = QH // KVH
TOK = 128
RUN = 64
NX, NY, NZ = 4, 8, 2
SCALE = math.log2(math.e) / math.sqrt(HD)
NEG = -1e6
KV_ROWS = 4 * RUN
Q_ROWS = 2 * GROUP * RUN
META = 16
CHUNKS = (
    (("OO", 0), ("OX", 0), ("OO", -1), ("OO", 1)),
    (("OX", -1), ("OX", 1), ("OO", -2), ("OO", 2)),
    (("OX", -2), ("OX", 2), ("ZO", 0), ("ZX", 0)),
    (("OO", -3), ("OO", 3), ("OX", -3), ("OX", 3)),
    (("ZO", -1), ("ZO", 1), ("ZX", -1), ("ZX", 1)),
    (("OO", 4), ("OX", 4), ("ZO", -2), ("ZO", 2)),
    (("ZX", -2), ("ZX", 2)),
    (("ZO", -3), ("ZO", 3), ("ZX", -3), ("ZX", 3)),
    (("ZO", 4), ("ZX", 4)),
)
FIRST = [sum(len(chunk) for chunk in CHUNKS[:i]) for i in range(len(CHUNKS))]
SLOT = {name: i for i, name in enumerate(name for chunk in CHUNKS for name in chunk)}
PLAN = (
    ("pass", "OO", 1), ("pass", "OX", 1),
    ("pass", "OO", 2), ("pass", "OX", 2),
    ("pass", "ZO", 0), ("pass", "ZX", 0), ("query",), ("wait", "OX", 0), ("attend", 0), ("attend", 1),
    ("pass", "OO", 3), ("pass", "OX", 3),
    ("pass", "ZO", 1), ("pass", "ZX", 1), ("attend", 2),
    ("far", "OO"), ("far", "OX"), ("attend", 3),
    ("pass", "ZO", 2), ("pass", "ZX", 2), ("attend", 4), ("attend", 5), ("attend", 6),
    ("wait", "ZO", 3), ("wait", "ZX", 3), ("wait", "ZO", 4), ("wait", "ZX", 4),
)
LAST = (7, 8)
X_STEP = {1: 1, 2: NX - 1, 3: 2}
X_BACK = {1: 2, 2: 1, 3: 3}


def nt(a, b):
    return lax.dot_general(a, b, (((1,), (1,)), ((), ())), preferred_element_type=F32)


def nn(a, b):
    return lax.dot_general(a, b, (((1,), (0,)), ((), ())), preferred_element_type=F32)


def lanes(x, n):
    return jnp.concatenate([x] * (n // HD), axis=1)


def fold(q, k, v, bias, m_ref, l_ref, a_ref, first):
    s = nt(q, k)
    if bias.shape[0] == 1:
        bias = jnp.broadcast_to(bias, (GROUP * RUN, bias.shape[1]))
    masked = s[: GROUP * RUN] + bias
    s = masked if s.shape[0] == GROUP * RUN else jnp.concatenate([masked, s[GROUP * RUN :]], axis=0)
    peak = jnp.max(s, axis=1, keepdims=True)
    if first:
        new = jnp.broadcast_to(peak, m_ref.shape)
    else:
        old = m_ref[...]
        new = jnp.maximum(old, peak)
    shift = new * SCALE
    p = jnp.exp2(s * SCALE - lanes(shift, s.shape[1]))
    total = sum((p[:, i : i + HD] for i in range(HD, s.shape[1], HD)), p[:, :HD])
    update = nn(p.astype(BF16), v)
    if first:
        l_ref[...] = total
        a_ref[...] = update
    else:
        shrink = jnp.exp2(old * SCALE - shift)
        l_ref[...] = l_ref[...] * shrink + total
        a_ref[...] = a_ref[...] * shrink + update
    m_ref[...] = new


def kernel(
    pos_hbm, q_hbm, k_hbm, v_hbm, out_ref, lse_ref,
    pos_ref, q_ref, k_ref, v_ref, kv, spare, qb, qspare, ob, osend, m, l, a,
    load_sem, kv_send, kv_recv, q_send, q_recv, o_send, o_recv,
):
    loads = [
        pltpu.make_async_copy(src, dst, load_sem.at[i])
        for i, (src, dst) in enumerate(((k_hbm, k_ref), (v_hbm, v_ref), (q_hbm, q_ref), (pos_hbm, pos_ref)))
    ]
    for load in loads:
        load.start()
    me = lax.axis_index("ctx")
    my_y, my_x, my_z = me // (NX * NZ), lax.rem(me // NZ, NX), lax.rem(me, NZ)
    head = lax.rem(my_x, 2)
    pair_step = 1 + head * (NX - 2)

    def at(dy, dx, dz):
        y, x, z = lax.rem(my_y + dy, NY), lax.rem(my_x + dx, NX), lax.rem(my_z + dz, NZ)
        return {"ctx": (y * NX + x) * NZ + z}

    up, down, across = at(1, 0, 0), at(NY - 1, 0, 0), at(0, 0, 1)
    beside, diagonal = at(0, pair_step, 0), at(0, pair_step, 1)
    above, below = at(1, pair_step, 0), at(NY - 1, pair_step, 0)
    row = {i: at(0, X_STEP[i], 0) for i in (1, 2, 3)}
    barrier = pltpu.get_barrier_semaphore()
    greet = (diagonal, across, row[3], above, below, up, down, row[1], row[2])
    for peer in greet:
        pl.semaphore_signal(barrier, inc=1, device_id=peer, device_id_type=MESH)

    loads[3].wait()
    number = lax.shift_right_logical(pos_ref[...], 6)
    low = jnp.minimum(number, 2 * RUN - 1 - number)
    lane = lax.broadcasted_iota(jnp.int32, (1, HD), 1)
    swapped = jnp.where((low == number) == (lane < RUN), 0.0, 1.0)
    meta = jnp.broadcast_to(low.astype(F32), (META, HD)).astype(BF16)
    turn = jnp.broadcast_to(swapped, (RUN, HD)).astype(BF16) > 0.5

    def columns(h, g, heads):
        return pl.ds(pl.multiple_of((h * heads + g) * HD, HD), HD)

    def half(ref, r, cols):
        return jnp.where(turn, ref[(1 - r) * RUN : (2 - r) * RUN, cols], ref[r * RUN : (r + 1) * RUN, cols])

    def stage_kv(h, dst):
        cols = columns(h, 0, 1)
        for r in range(2):
            dst[r * RUN : (r + 1) * RUN, :] = half(k_ref, r, cols)
            dst[(2 + r) * RUN : (3 + r) * RUN, :] = half(v_ref, r, cols)
        dst[KV_ROWS:, :] = meta

    def stage_q(h, dst):
        for r in range(2):
            for g in range(GROUP):
                base = (r * GROUP + g) * RUN
                dst[base : base + RUN, :] = half(q_ref, r, columns(h, g, GROUP))
        dst[Q_ROWS:, :] = meta

    started = []

    def kv_copy(src, slot, device):
        return pltpu.make_async_remote_copy(
            src_ref=src, dst_ref=kv.at[slot], send_sem=kv_send.at[slot], recv_sem=kv_recv.at[slot],
            device_id=device, device_id_type=MESH,
        )

    def send_kv(src, name, device):
        copy = kv_copy(src, SLOT[name], device)
        copy.start()
        started.append(copy)

    def got_kv(*name):
        if name != ("OO", 0):
            kv_copy(kv.at[SLOT[name]], SLOT[name], up).wait_recv()

    def pass_on(stream, step):
        for y, device in ((-step, up), (step, down)):
            if step or device is up:
                got_kv(stream, y)
            after = y - 1 if device is up else y + 1
            block = kv.at[SLOT[stream, y]]
            if step < 3:
                send_kv(block, (stream, after), device)
            elif stream == ("OO" if device is up else "OX"):
                send_kv(block, (stream, 4), device)

    def far(stream):
        got_kv(stream, 4)
        send_kv(kv.at[SLOT[stream, 4]], ("Z" + stream[1], 4), across)

    def wait(stream, step):
        for y in (-step, step) if 0 < step < 4 else (step,):
            got_kv(stream, y)

    def q_copy(i):
        return pltpu.make_async_remote_copy(
            src_ref=qb.at[0] if i == 3 else qspare, dst_ref=qb.at[X_BACK[i]],
            send_sem=q_send.at[i], recv_sem=q_recv.at[X_BACK[i]],
            device_id=row[i], device_id_type=MESH,
        )

    def o_copy(i):
        return pltpu.make_async_remote_copy(
            src_ref=osend.at[i], dst_ref=ob.at[X_BACK[i]],
            send_sem=o_send.at[i], recv_sem=o_recv.at[X_BACK[i]],
            device_id=row[i], device_id_type=MESH,
        )

    lane64 = lane < RUN

    def attend(chunk, slots=range(NX)):
        first = chunk == 0
        s0, size = FIRST[chunk], len(CHUNKS[chunk])
        wide = size * RUN
        k1, k2, v1, v2 = [
            kv[s0 : s0 + size, i * RUN : (i + 1) * RUN, :].reshape(wide, HD) for i in range(4)
        ]
        run = [kv[s0 + i, KV_ROWS:, :].astype(F32)[0:1] for i in range(size)]
        theirs = jnp.concatenate(
            [jnp.where(lane64, run[i], run[i + 1]) for i in range(0, size, 2)], axis=1
        )
        token = lax.rem(lax.broadcasted_iota(jnp.int32, (GROUP * RUN, wide), 0), RUN)
        column = lax.rem(lax.broadcasted_iota(jnp.int32, (GROUP * RUN, wide), 1), RUN)
        triangle = jnp.where(column <= token, 0.0, NEG)
        for c in slots:
            mine = lanes(qb[c, Q_ROWS:, :].astype(F32)[0:1], wide)
            bias1 = jnp.where(theirs < mine, 0.0, NEG)
            bias2 = jnp.where(theirs > mine, 0.0, NEG)
            if first and c < 3:
                bias1 = jnp.where(theirs == mine, triangle, bias1)
                bias2 = jnp.where(theirs == mine, triangle, bias2)
            second = slice(GROUP * RUN, Q_ROWS)
            fold(qb[c, :Q_ROWS, :], k1, v1, bias1, m.at[c], l.at[c], a.at[c], first)
            fold(qb[c, second, :], k2, v2, bias2, m.at[c, second], l.at[c, second], a.at[c, second], False)

    eye = lax.broadcasted_iota(jnp.int32, (HD, HD), 0) == lax.broadcasted_iota(jnp.int32, (HD, HD), 1)

    def close(c, dst):
        total = jnp.sum(l[c], axis=1, keepdims=True)
        dst[:Q_ROWS, :] = (a[c] * (1.0 / total)).astype(BF16)
        logs = m[c] * SCALE + jnp.log2(total)
        rows = []
        for g in range(GROUP):
            starts = [(r * GROUP + g) * RUN for r in range(2)]
            both = jnp.concatenate([logs[i : i + RUN] for i in starts], axis=0)
            rows.append(jnp.sum(jnp.where(eye, both, 0.0), axis=0, keepdims=True))
        rest = jnp.concatenate(rows, axis=0)
        pieces = []
        for unused in range(3):
            piece = rest.astype(BF16).astype(F32)
            rest = rest - piece
            pieces.append(piece)
        pieces.append(jnp.zeros_like(rest))
        dst[Q_ROWS:, :] = jnp.concatenate(pieces, axis=0).astype(BF16)

    to_row = lax.broadcasted_iota(jnp.int32, (HD, HD), 0)
    from_row = lax.broadcasted_iota(jnp.int32, (HD, HD), 1)
    place = to_row == jnp.where(swapped > 0.5, lax.bitwise_xor(from_row, RUN), from_row)

    def merge(h, sources):
        logs = []
        for i in sources:
            t = ob[i, Q_ROWS:, :].astype(F32)
            logs.append(t[0:4] + t[4:8] + t[8:12])
        top = functools.reduce(jnp.maximum, logs)
        weights = [jnp.exp2(x - top) for x in logs]
        total = sum(weights[1:], weights[0])
        weights = [w / total for w in weights]
        for g in range(GROUP):
            left, right = [], []
            for w, i in zip(weights, sources):
                spread = jnp.where(place, w[g : g + 1, :], 0.0)
                high = spread.astype(BF16)
                left += [high, (spread - high.astype(F32)).astype(BF16)]
                part = [ob[i, (r * GROUP + g) * RUN : (r * GROUP + g + 1) * RUN, :] for r in range(2)]
                right += part + part
            o = nn(jnp.concatenate(left, axis=1), jnp.concatenate(right, axis=0))
            out_ref[:, columns(h, g, GROUP)] = o.astype(BF16)
        whole = (top + jnp.log2(total)) * math.log(2.0)
        turned = jnp.concatenate([whole[:, RUN:], whole[:, :RUN]], axis=1)
        return jnp.where(swapped > 0.5, turned, whole)

    own = kv.at[SLOT["OO", 0]]
    loads[0].wait()
    loads[1].wait()
    stage_kv(head, own)
    stage_kv(1 - head, spare)
    loads[2].wait()
    stage_q(1 - head, qspare)
    stage_q(head, qb.at[0])
    pl.semaphore_wait(barrier, len(greet))
    send_kv(own, ("ZO", 0), across)
    send_kv(spare, ("ZX", 0), diagonal)
    send_kv(own, ("OO", -1), up)
    send_kv(own, ("OO", 1), down)
    send_kv(spare, ("OX", 0), beside)
    send_kv(spare, ("OX", -1), above)
    send_kv(spare, ("OX", 1), below)
    for i in (3, 1, 2):
        q_copy(i).start()
    for what, *rest in PLAN:
        if what == "query":
            for i in (1, 2, 3):
                q_copy(i).wait_recv()
        else:
            {"pass": pass_on, "far": far, "wait": wait, "attend": attend}[what](*rest)
    for i in (3, 1, 2, 0):
        for chunk in LAST:
            attend(chunk, (i,))
        if i:
            close(i, osend.at[i])
            o_copy(i).start()
        else:
            close(0, ob.at[0])
    o_copy(3).wait_recv()
    mine = merge(head, (0, 3))
    o_copy(1).wait_recv()
    o_copy(2).wait_recv()
    other = merge(1 - head, (1, 2))
    even = jnp.where(head == 0, 1.0, 0.0)
    lse_ref[0:GROUP, :] = jnp.where(even > 0.5, mine, other)
    lse_ref[GROUP:, :] = jnp.where(even > 0.5, other, mine)
    for copy in started:
        copy.wait_send()
    for i in (1, 2, 3):
        q_copy(i).wait_send()
        o_copy(i).wait_send()


def shards(queries, keys, values, positions):
    vmem = pl.BlockSpec(memory_space=pltpu.VMEM)
    hbm = pl.BlockSpec(memory_space=pltpu.HBM)
    state = pltpu.VMEM((NX, Q_ROWS, HD), F32)
    shared = pltpu.VMEM((NX, Q_ROWS + META, HD), BF16)
    blocks = len(SLOT)
    inputs = (positions.reshape(1, TOK), queries, keys, values)
    return pl.pallas_call(
        kernel,
        name="ring_attention",
        out_shape=(
            jax.ShapeDtypeStruct((TOK, QH * HD), BF16),
            jax.ShapeDtypeStruct((QH, TOK), F32),
        ),
        in_specs=[hbm, hbm, hbm, hbm],
        out_specs=(vmem, vmem),
        scratch_shapes=[
            pltpu.VMEM((1, TOK), jnp.int32),
            pltpu.VMEM((TOK, QH * HD), BF16),
            pltpu.VMEM((TOK, KVH * HD), BF16),
            pltpu.VMEM((TOK, KVH * HD), BF16),
            pltpu.VMEM((blocks, KV_ROWS + META, HD), BF16),
            pltpu.VMEM((KV_ROWS + META, HD), BF16),
            shared,
            pltpu.VMEM((Q_ROWS + META, HD), BF16),
            shared,
            shared,
            state,
            state,
            state,
            pltpu.SemaphoreType.DMA((4,)),
            pltpu.SemaphoreType.DMA((blocks,)),
            pltpu.SemaphoreType.DMA((blocks,)),
            pltpu.SemaphoreType.DMA((NX,)),
            pltpu.SemaphoreType.DMA((NX,)),
            pltpu.SemaphoreType.DMA((NX,)),
            pltpu.SemaphoreType.DMA((NX,)),
        ],
        compiler_params=pltpu.CompilerParams(
            collective_id=0, has_side_effects=True, vmem_limit_bytes=40 * 2**20
        ),
    )(*(pltpu.with_memory_space_constraint(x, pltpu.HBM) for x in inputs))


def solution(mesh):
    return jax.shard_map(
        shards,
        mesh=mesh,
        in_specs=(
            P(("dp", "ctx"), None),
            P(("dp", "ctx"), None),
            P(("dp", "ctx"), None),
            P(("dp", "ctx")),
        ),
        out_specs=(P(("dp", "ctx"), None), P(None, ("dp", "ctx"))),
        check_vma=False,
    )
```

```python
import functools
import math

import jax
import jax.numpy as jnp
from jax import lax
from jax.experimental import pallas as pl
from jax.experimental.pallas import tpu as pltpu
from jax.sharding import PartitionSpec as P

MESH = pl.DeviceIdType.MESH
F32 = jnp.float32
BF16 = jnp.bfloat16
HD = 128
QH = 8
KVH = 2
GROUP = QH // KVH
TOK = 128
RUN = 64
NX, NY, NZ = 4, 8, 2
SCALE = math.log2(math.e) / math.sqrt(HD)
NEG = -1e6
KV_ROWS = 4 * RUN
Q_ROWS = 2 * GROUP * RUN
META = 8
TAIL = 16
CHUNKS = (
    (("OO", 0), ("OX", 0), ("OO", -1), ("OO", 1)),
    (("OX", -1), ("OX", 1), ("OO", -2), ("OO", 2)),
    (("OX", -2), ("OX", 2), ("ZO", 0), ("ZX", 0)),
    (("OO", -3), ("OO", 3), ("OX", -3), ("OX", 3)),
    (("ZO", -1), ("ZO", 1), ("ZX", -1), ("ZX", 1)),
    (("OO", 4), ("OX", 4), ("ZO", -2), ("ZO", 2)),
    (("ZX", -2), ("ZX", 2)),
    (("ZO", -3), ("ZO", 3), ("ZX", -3), ("ZX", 3)),
    (("ZO", 4), ("ZX", 4)),
)
FIRST = [sum(len(chunk) for chunk in CHUNKS[:i]) for i in range(len(CHUNKS))]
SLOT = {name: i for i, name in enumerate(name for chunk in CHUNKS for name in chunk)}
PLAN = (
    ("pass", "OO", 1), ("pass", "OX", 1),
    ("pass", "OO", 2), ("pass", "OX", 2),
    ("pass", "ZO", 0), ("pass", "ZX", 0), ("query",), ("wait", "OX", 0), ("attend", 0), ("attend", 1),
    ("pass", "OO", 3), ("pass", "OX", 3),
    ("pass", "ZO", 1), ("pass", "ZX", 1), ("attend", 2),
    ("far", "OO"), ("far", "OX"), ("attend", 3),
    ("pass", "ZO", 2), ("pass", "ZX", 2), ("attend", 4), ("attend", 5), ("attend", 6),
    ("wait", "ZO", 3), ("wait", "ZX", 3), ("wait", "ZO", 4), ("wait", "ZX", 4),
)
LAST = (7, 8)
X_STEP = {1: 1, 2: NX - 1, 3: 2}
X_BACK = {1: 2, 2: 1, 3: 3}


def nt(a, b):
    return lax.dot_general(a, b, (((1,), (1,)), ((), ())), preferred_element_type=F32)


def nn(a, b):
    return lax.dot_general(a, b, (((1,), (0,)), ((), ())), preferred_element_type=F32)


def lanes(x, n):
    return jnp.concatenate([x] * (n // HD), axis=1)


def fold(q, k, v, bias, m_ref, l_ref, a_ref, first):
    s = nt(q, k)
    if bias.shape[0] == 1:
        bias = jnp.broadcast_to(bias, (GROUP * RUN, bias.shape[1]))
    masked = s[: GROUP * RUN] + bias
    s = masked if s.shape[0] == GROUP * RUN else jnp.concatenate([masked, s[GROUP * RUN :]], axis=0)
    peak = jnp.max(s, axis=1, keepdims=True)
    if first:
        new = jnp.broadcast_to(peak, m_ref.shape)
    else:
        old = m_ref[...]
        new = jnp.maximum(old, peak)
    shift = new * SCALE
    p = jnp.exp2(s * SCALE - lanes(shift, s.shape[1]))
    total = sum((p[:, i : i + HD] for i in range(HD, s.shape[1], HD)), p[:, :HD])
    update = nn(p.astype(BF16), v)
    if first:
        l_ref[...] = total
        a_ref[...] = update
    else:
        shrink = jnp.exp2(old * SCALE - shift)
        l_ref[...] = l_ref[...] * shrink + total
        a_ref[...] = a_ref[...] * shrink + update
    m_ref[...] = new


def kernel(
    pos_hbm, q_hbm, k_hbm, v_hbm, out_ref, lse_ref,
    pos_ref, q_ref, k_ref, v_ref, kv, spare, qb, qspare, ob, osend, m, l, a,
    load_sem, kv_send, kv_recv, q_send, q_recv, o_send, o_recv,
):
    loads = [
        pltpu.make_async_copy(src, dst, load_sem.at[i])
        for i, (src, dst) in enumerate(((k_hbm, k_ref), (v_hbm, v_ref), (q_hbm, q_ref), (pos_hbm, pos_ref)))
    ]
    for load in loads:
        load.start()
    me = lax.axis_index("ctx")
    my_y, my_x, my_z = me // (NX * NZ), lax.rem(me // NZ, NX), lax.rem(me, NZ)
    head = lax.rem(my_x, 2)
    pair_step = 1 + head * (NX - 2)

    def at(dy, dx, dz):
        y, x, z = lax.rem(my_y + dy, NY), lax.rem(my_x + dx, NX), lax.rem(my_z + dz, NZ)
        return {"ctx": (y * NX + x) * NZ + z}

    up, down, across = at(1, 0, 0), at(NY - 1, 0, 0), at(0, 0, 1)
    beside, diagonal = at(0, pair_step, 0), at(0, pair_step, 1)
    above, below = at(1, pair_step, 0), at(NY - 1, pair_step, 0)
    row = {i: at(0, X_STEP[i], 0) for i in (1, 2, 3)}
    barrier = pltpu.get_barrier_semaphore()
    greet = (diagonal, across, row[3], above, below, up, down, row[1], row[2])
    for peer in greet:
        pl.semaphore_signal(barrier, inc=1, device_id=peer, device_id_type=MESH)

    loads[3].wait()
    number = lax.shift_right_logical(pos_ref[...], 6)
    low = jnp.minimum(number, 2 * RUN - 1 - number)
    lane = lax.broadcasted_iota(jnp.int32, (1, HD), 1)
    swapped = jnp.where((low == number) == (lane < RUN), 0.0, 1.0)
    meta = jnp.broadcast_to(low.astype(F32), (META, HD)).astype(BF16)
    turn = jnp.broadcast_to(swapped, (RUN, HD)).astype(BF16) > 0.5

    def columns(h, g, heads):
        return pl.ds(pl.multiple_of((h * heads + g) * HD, HD), HD)

    def half(ref, r, cols):
        return jnp.where(turn, ref[(1 - r) * RUN : (2 - r) * RUN, cols], ref[r * RUN : (r + 1) * RUN, cols])

    def stage_kv(h, dst):
        cols = columns(h, 0, 1)
        for r in range(2):
            dst[r * RUN : (r + 1) * RUN, :] = half(k_ref, r, cols)
            dst[(2 + r) * RUN : (3 + r) * RUN, :] = half(v_ref, r, cols)
        dst[KV_ROWS:, :] = meta

    def stage_q(h, dst):
        for r in range(2):
            for g in range(GROUP):
                base = (r * GROUP + g) * RUN
                dst[base : base + RUN, :] = half(q_ref, r, columns(h, g, GROUP))
        dst[Q_ROWS:, :] = meta

    started = []

    def kv_copy(src, slot, device):
        return pltpu.make_async_remote_copy(
            src_ref=src, dst_ref=kv.at[slot], send_sem=kv_send.at[slot], recv_sem=kv_recv.at[slot],
            device_id=device, device_id_type=MESH,
        )

    def send_kv(src, name, device):
        copy = kv_copy(src, SLOT[name], device)
        copy.start()
        started.append(copy)

    def got_kv(*name):
        if name != ("OO", 0):
            kv_copy(kv.at[SLOT[name]], SLOT[name], up).wait_recv()

    def pass_on(stream, step):
        for y, device in ((-step, up), (step, down)):
            if step or device is up:
                got_kv(stream, y)
            after = y - 1 if device is up else y + 1
            block = kv.at[SLOT[stream, y]]
            if step < 3:
                send_kv(block, (stream, after), device)
            elif stream == ("OO" if device is up else "OX"):
                send_kv(block, (stream, 4), device)

    def far(stream):
        got_kv(stream, 4)
        send_kv(kv.at[SLOT[stream, 4]], ("Z" + stream[1], 4), across)

    def wait(stream, step):
        for y in (-step, step) if 0 < step < 4 else (step,):
            got_kv(stream, y)

    def q_copy(i):
        return pltpu.make_async_remote_copy(
            src_ref=qb.at[0] if i == 3 else qspare, dst_ref=qb.at[X_BACK[i]],
            send_sem=q_send.at[i], recv_sem=q_recv.at[X_BACK[i]],
            device_id=row[i], device_id_type=MESH,
        )

    def o_copy(i):
        return pltpu.make_async_remote_copy(
            src_ref=osend.at[i], dst_ref=ob.at[X_BACK[i]],
            send_sem=o_send.at[i], recv_sem=o_recv.at[X_BACK[i]],
            device_id=row[i], device_id_type=MESH,
        )

    lane64 = lane < RUN

    def attend(chunk, slots=range(NX)):
        first = chunk == 0
        s0, size = FIRST[chunk], len(CHUNKS[chunk])
        wide = size * RUN
        k1, k2, v1, v2 = [
            kv[s0 : s0 + size, i * RUN : (i + 1) * RUN, :].reshape(wide, HD) for i in range(4)
        ]
        run = [kv[s0 + i, KV_ROWS:, :].astype(F32)[0:1] for i in range(size)]
        theirs = jnp.concatenate(
            [jnp.where(lane64, run[i], run[i + 1]) for i in range(0, size, 2)], axis=1
        )
        token = lax.rem(lax.broadcasted_iota(jnp.int32, (GROUP * RUN, wide), 0), RUN)
        column = lax.rem(lax.broadcasted_iota(jnp.int32, (GROUP * RUN, wide), 1), RUN)
        triangle = jnp.where(column <= token, 0.0, NEG)
        for c in slots:
            mine = lanes(qb[c, Q_ROWS:, :].astype(F32)[0:1], wide)
            bias1 = jnp.where(theirs < mine, 0.0, NEG)
            bias2 = jnp.where(theirs > mine, 0.0, NEG)
            if first and c < 3:
                bias1 = jnp.where(theirs == mine, triangle, bias1)
                bias2 = jnp.where(theirs == mine, triangle, bias2)
            second = slice(GROUP * RUN, Q_ROWS)
            fold(qb[c, :Q_ROWS, :], k1, v1, bias1, m.at[c], l.at[c], a.at[c], first)
            fold(qb[c, second, :], k2, v2, bias2, m.at[c, second], l.at[c, second], a.at[c, second], False)

    eye = lax.broadcasted_iota(jnp.int32, (HD, HD), 0) == lax.broadcasted_iota(jnp.int32, (HD, HD), 1)

    def close(c, dst):
        total = jnp.sum(l[c], axis=1, keepdims=True)
        dst[:Q_ROWS, :] = (a[c] * (1.0 / total)).astype(BF16)
        logs = m[c] * SCALE + jnp.log2(total)
        rows = []
        for g in range(GROUP):
            starts = [(r * GROUP + g) * RUN for r in range(2)]
            both = jnp.concatenate([logs[i : i + RUN] for i in starts], axis=0)
            rows.append(jnp.sum(jnp.where(eye, both, 0.0), axis=0, keepdims=True))
        rest = jnp.concatenate(rows, axis=0)
        pieces = []
        for unused in range(3):
            piece = rest.astype(BF16).astype(F32)
            rest = rest - piece
            pieces.append(piece)
        pieces.append(jnp.zeros_like(rest))
        dst[Q_ROWS:, :] = jnp.concatenate(pieces, axis=0).astype(BF16)

    to_row = lax.broadcasted_iota(jnp.int32, (HD, HD), 0)
    from_row = lax.broadcasted_iota(jnp.int32, (HD, HD), 1)
    place = to_row == jnp.where(swapped > 0.5, lax.bitwise_xor(from_row, RUN), from_row)

    def merge(h, sources):
        logs = []
        for i in sources:
            t = ob[i, Q_ROWS:, :].astype(F32)
            logs.append(t[0:4] + t[4:8] + t[8:12])
        top = functools.reduce(jnp.maximum, logs)
        weights = [jnp.exp2(x - top) for x in logs]
        total = sum(weights[1:], weights[0])
        weights = [w / total for w in weights]
        for g in range(GROUP):
            left, right = [], []
            for w, i in zip(weights, sources):
                spread = jnp.where(place, w[g : g + 1, :], 0.0)
                high = spread.astype(BF16)
                left += [high, (spread - high.astype(F32)).astype(BF16)]
                part = [ob[i, (r * GROUP + g) * RUN : (r * GROUP + g + 1) * RUN, :] for r in range(2)]
                right += part + part
            o = nn(jnp.concatenate(left, axis=1), jnp.concatenate(right, axis=0))
            out_ref[:, columns(h, g, GROUP)] = o.astype(BF16)
        whole = (top + jnp.log2(total)) * math.log(2.0)
        turned = jnp.concatenate([whole[:, RUN:], whole[:, :RUN]], axis=1)
        return jnp.where(swapped > 0.5, turned, whole)

    own = kv.at[SLOT["OO", 0]]
    loads[0].wait()
    loads[1].wait()
    stage_kv(head, own)
    stage_kv(1 - head, spare)
    loads[2].wait()
    stage_q(1 - head, qspare)
    stage_q(head, qb.at[0])
    pl.semaphore_wait(barrier, len(greet))
    send_kv(own, ("ZO", 0), across)
    send_kv(spare, ("ZX", 0), diagonal)
    send_kv(own, ("OO", -1), up)
    send_kv(own, ("OO", 1), down)
    send_kv(spare, ("OX", 0), beside)
    send_kv(spare, ("OX", -1), above)
    send_kv(spare, ("OX", 1), below)
    for i in (3, 1, 2):
        q_copy(i).start()
    for what, *rest in PLAN:
        if what == "query":
            for i in (1, 2, 3):
                q_copy(i).wait_recv()
        else:
            {"pass": pass_on, "far": far, "wait": wait, "attend": attend}[what](*rest)
    for i in (3, 1, 2, 0):
        for chunk in LAST:
            attend(chunk, (i,))
        if i:
            close(i, osend.at[i])
            o_copy(i).start()
        else:
            close(0, ob.at[0])
    o_copy(3).wait_recv()
    mine = merge(head, (0, 3))
    o_copy(1).wait_recv()
    o_copy(2).wait_recv()
    other = merge(1 - head, (1, 2))
    even = jnp.where(head == 0, 1.0, 0.0)
    lse_ref[0:GROUP, :] = jnp.where(even > 0.5, mine, other)
    lse_ref[GROUP:, :] = jnp.where(even > 0.5, other, mine)
    for copy in started:
        copy.wait_send()
    for i in (1, 2, 3):
        q_copy(i).wait_send()
        o_copy(i).wait_send()


def shards(queries, keys, values, positions):
    vmem = pl.BlockSpec(memory_space=pltpu.VMEM)
    hbm = pl.BlockSpec(memory_space=pltpu.HBM)
    state = pltpu.VMEM((NX, Q_ROWS, HD), F32)
    shared = pltpu.VMEM((NX, Q_ROWS + META, HD), BF16)
    partial = pltpu.VMEM((NX, Q_ROWS + TAIL, HD), BF16)
    blocks = len(SLOT)
    inputs = (positions.reshape(1, TOK), queries, keys, values)
    return pl.pallas_call(
        kernel,
        name="ring_attention",
        out_shape=(
            jax.ShapeDtypeStruct((TOK, QH * HD), BF16),
            jax.ShapeDtypeStruct((QH, TOK), F32),
        ),
        in_specs=[hbm, hbm, hbm, hbm],
        out_specs=(vmem, vmem),
        scratch_shapes=[
            pltpu.VMEM((1, TOK), jnp.int32),
            pltpu.VMEM((TOK, QH * HD), BF16),
            pltpu.VMEM((TOK, KVH * HD), BF16),
            pltpu.VMEM((TOK, KVH * HD), BF16),
            pltpu.VMEM((blocks, KV_ROWS + META, HD), BF16),
            pltpu.VMEM((KV_ROWS + META, HD), BF16),
            shared,
            pltpu.VMEM((Q_ROWS + META, HD), BF16),
            partial,
            partial,
            state,
            state,
            state,
            pltpu.SemaphoreType.DMA((4,)),
            pltpu.SemaphoreType.DMA((blocks,)),
            pltpu.SemaphoreType.DMA((blocks,)),
            pltpu.SemaphoreType.DMA((NX,)),
            pltpu.SemaphoreType.DMA((NX,)),
            pltpu.SemaphoreType.DMA((NX,)),
            pltpu.SemaphoreType.DMA((NX,)),
        ],
        compiler_params=pltpu.CompilerParams(
            collective_id=0, has_side_effects=True, vmem_limit_bytes=40 * 2**20
        ),
    )(*(pltpu.with_memory_space_constraint(x, pltpu.HBM) for x in inputs))


def solution(mesh):
    return jax.shard_map(
        shards,
        mesh=mesh,
        in_specs=(
            P(("dp", "ctx"), None),
            P(("dp", "ctx"), None),
            P(("dp", "ctx"), None),
            P(("dp", "ctx")),
        ),
        out_specs=(P(("dp", "ctx"), None), P(None, ("dp", "ctx"))),
        check_vma=False,
    )
```

```python
import functools
import math

import jax
import jax.numpy as jnp
from jax import lax
from jax.experimental import pallas as pl
from jax.experimental.pallas import tpu as pltpu
from jax.sharding import PartitionSpec as P

MESH = pl.DeviceIdType.MESH
F32 = jnp.float32
BF16 = jnp.bfloat16
HD = 128
QH = 8
KVH = 2
GROUP = QH // KVH
TOK = 128
RUN = 64
NX, NY, NZ = 4, 8, 2
SCALE = math.log2(math.e) / math.sqrt(HD)
NEG = -1e6
KV_ROWS = 4 * RUN
Q_ROWS = 2 * GROUP * RUN
META = 8
TAIL = 16
CHUNKS = (
    (("OO", 0), ("OX", 0), ("OO", -1), ("OO", 1)),
    (("OX", -1), ("OX", 1), ("OO", -2), ("OO", 2)),
    (("OX", -2), ("OX", 2), ("ZO", 0), ("ZX", 0)),
    (("OO", -3), ("OO", 3), ("OX", -3), ("OX", 3)),
    (("ZO", -1), ("ZO", 1), ("ZX", -1), ("ZX", 1)),
    (("OO", 4), ("OX", 4), ("ZO", -2), ("ZO", 2)),
    (("ZX", -2), ("ZX", 2)),
    (("ZO", -3), ("ZO", 3), ("ZX", -3), ("ZX", 3)),
    (("ZO", 4), ("ZX", 4)),
)
FIRST = [sum(len(chunk) for chunk in CHUNKS[:i]) for i in range(len(CHUNKS))]
SLOT = {name: i for i, name in enumerate(name for chunk in CHUNKS for name in chunk)}
PLAN = (
    ("pass", "OO", 1), ("pass", "OX", 1),
    ("pass", "OO", 2), ("pass", "OX", 2),
    ("pass", "ZO", 0), ("pass", "ZX", 0), ("query",), ("wait", "OX", 0), ("attend", 0), ("attend", 1),
    ("pass", "OO", 3), ("pass", "OX", 3),
    ("pass", "ZO", 1), ("pass", "ZX", 1),
    ("far", "OO"), ("far", "OX"), ("attend", 2), ("attend", 3),
    ("pass", "ZO", 2), ("pass", "ZX", 2), ("attend", 4), ("attend", 5), ("attend", 6),
    ("wait", "ZO", 3), ("wait", "ZX", 3), ("wait", "ZO", 4), ("wait", "ZX", 4),
)
LAST = (7, 8)
X_STEP = {1: 1, 2: NX - 1, 3: 2}
X_BACK = {1: 2, 2: 1, 3: 3}


def nt(a, b):
    return lax.dot_general(a, b, (((1,), (1,)), ((), ())), preferred_element_type=F32)


def nn(a, b):
    return lax.dot_general(a, b, (((1,), (0,)), ((), ())), preferred_element_type=F32)


def lanes(x, n):
    return jnp.concatenate([x] * (n // HD), axis=1)


def fold(q, k, v, bias, m_ref, l_ref, a_ref, first):
    s = nt(q, k)
    if bias.shape[0] == 1:
        bias = jnp.broadcast_to(bias, (GROUP * RUN, bias.shape[1]))
    masked = s[: GROUP * RUN] + bias
    s = masked if s.shape[0] == GROUP * RUN else jnp.concatenate([masked, s[GROUP * RUN :]], axis=0)
    peak = jnp.max(s, axis=1, keepdims=True)
    if first:
        new = jnp.broadcast_to(peak, m_ref.shape)
    else:
        old = m_ref[...]
        new = jnp.maximum(old, peak)
    shift = new * SCALE
    p = jnp.exp2(s * SCALE - lanes(shift, s.shape[1]))
    total = sum((p[:, i : i + HD] for i in range(HD, s.shape[1], HD)), p[:, :HD])
    update = nn(p.astype(BF16), v)
    if first:
        l_ref[...] = total
        a_ref[...] = update
    else:
        shrink = jnp.exp2(old * SCALE - shift)
        l_ref[...] = l_ref[...] * shrink + total
        a_ref[...] = a_ref[...] * shrink + update
    m_ref[...] = new


def kernel(
    pos_hbm, q_hbm, k_hbm, v_hbm, out_ref, lse_ref,
    pos_ref, q_ref, k_ref, v_ref, kv, spare, qb, qspare, ob, osend, m, l, a,
    load_sem, kv_send, kv_recv, q_send, q_recv, o_send, o_recv,
):
    loads = [
        pltpu.make_async_copy(src, dst, load_sem.at[i])
        for i, (src, dst) in enumerate(((k_hbm, k_ref), (v_hbm, v_ref), (q_hbm, q_ref), (pos_hbm, pos_ref)))
    ]
    for load in loads:
        load.start()
    me = lax.axis_index("ctx")
    my_y, my_x, my_z = me // (NX * NZ), lax.rem(me // NZ, NX), lax.rem(me, NZ)
    head = lax.rem(my_x, 2)
    pair_step = 1 + head * (NX - 2)

    def at(dy, dx, dz):
        y, x, z = lax.rem(my_y + dy, NY), lax.rem(my_x + dx, NX), lax.rem(my_z + dz, NZ)
        return {"ctx": (y * NX + x) * NZ + z}

    up, down, across = at(1, 0, 0), at(NY - 1, 0, 0), at(0, 0, 1)
    beside, diagonal = at(0, pair_step, 0), at(0, pair_step, 1)
    above, below = at(1, pair_step, 0), at(NY - 1, pair_step, 0)
    row = {i: at(0, X_STEP[i], 0) for i in (1, 2, 3)}
    barrier = pltpu.get_barrier_semaphore()
    greet = (diagonal, across, row[3], above, below, up, down, row[1], row[2])
    for peer in greet:
        pl.semaphore_signal(barrier, inc=1, device_id=peer, device_id_type=MESH)

    loads[3].wait()
    number = lax.shift_right_logical(pos_ref[...], 6)
    low = jnp.minimum(number, 2 * RUN - 1 - number)
    lane = lax.broadcasted_iota(jnp.int32, (1, HD), 1)
    swapped = jnp.where((low == number) == (lane < RUN), 0.0, 1.0)
    meta = jnp.broadcast_to(low.astype(F32), (META, HD)).astype(BF16)
    turn = jnp.broadcast_to(swapped, (RUN, HD)).astype(BF16) > 0.5

    def columns(h, g, heads):
        return pl.ds(pl.multiple_of((h * heads + g) * HD, HD), HD)

    def half(ref, r, cols):
        return jnp.where(turn, ref[(1 - r) * RUN : (2 - r) * RUN, cols], ref[r * RUN : (r + 1) * RUN, cols])

    def stage_kv(h, dst):
        cols = columns(h, 0, 1)
        for r in range(2):
            dst[r * RUN : (r + 1) * RUN, :] = half(k_ref, r, cols)
            dst[(2 + r) * RUN : (3 + r) * RUN, :] = half(v_ref, r, cols)
        dst[KV_ROWS:, :] = meta

    def stage_q(h, dst):
        for r in range(2):
            for g in range(GROUP):
                base = (r * GROUP + g) * RUN
                dst[base : base + RUN, :] = half(q_ref, r, columns(h, g, GROUP))
        dst[Q_ROWS:, :] = meta

    started = []

    def kv_copy(src, slot, device):
        return pltpu.make_async_remote_copy(
            src_ref=src, dst_ref=kv.at[slot], send_sem=kv_send.at[slot], recv_sem=kv_recv.at[slot],
            device_id=device, device_id_type=MESH,
        )

    def send_kv(src, name, device):
        copy = kv_copy(src, SLOT[name], device)
        copy.start()
        started.append(copy)

    def got_kv(*name):
        if name != ("OO", 0):
            kv_copy(kv.at[SLOT[name]], SLOT[name], up).wait_recv()

    def pass_on(stream, step):
        for y, device in ((-step, up), (step, down)):
            if step or device is up:
                got_kv(stream, y)
            after = y - 1 if device is up else y + 1
            block = kv.at[SLOT[stream, y]]
            if step < 3:
                send_kv(block, (stream, after), device)
            elif stream == ("OO" if device is up else "OX"):
                send_kv(block, (stream, 4), device)

    def far(stream):
        got_kv(stream, 4)
        send_kv(kv.at[SLOT[stream, 4]], ("Z" + stream[1], 4), across)

    def wait(stream, step):
        for y in (-step, step) if 0 < step < 4 else (step,):
            got_kv(stream, y)

    def q_copy(i):
        return pltpu.make_async_remote_copy(
            src_ref=qb.at[0] if i == 3 else qspare, dst_ref=qb.at[X_BACK[i]],
            send_sem=q_send.at[i], recv_sem=q_recv.at[X_BACK[i]],
            device_id=row[i], device_id_type=MESH,
        )

    def o_copy(i):
        return pltpu.make_async_remote_copy(
            src_ref=osend.at[i], dst_ref=ob.at[X_BACK[i]],
            send_sem=o_send.at[i], recv_sem=o_recv.at[X_BACK[i]],
            device_id=row[i], device_id_type=MESH,
        )

    lane64 = lane < RUN

    def attend(chunk, slots=range(NX)):
        first = chunk == 0
        s0, size = FIRST[chunk], len(CHUNKS[chunk])
        wide = size * RUN
        k1, k2, v1, v2 = [
            kv[s0 : s0 + size, i * RUN : (i + 1) * RUN, :].reshape(wide, HD) for i in range(4)
        ]
        run = [kv[s0 + i, KV_ROWS:, :].astype(F32)[0:1] for i in range(size)]
        theirs = jnp.concatenate(
            [jnp.where(lane64, run[i], run[i + 1]) for i in range(0, size, 2)], axis=1
        )
        token = lax.rem(lax.broadcasted_iota(jnp.int32, (GROUP * RUN, wide), 0), RUN)
        column = lax.rem(lax.broadcasted_iota(jnp.int32, (GROUP * RUN, wide), 1), RUN)
        triangle = jnp.where(column <= token, 0.0, NEG)
        for c in slots:
            mine = lanes(qb[c, Q_ROWS:, :].astype(F32)[0:1], wide)
            bias1 = jnp.where(theirs < mine, 0.0, NEG)
            bias2 = jnp.where(theirs > mine, 0.0, NEG)
            if first and c < 3:
                bias1 = jnp.where(theirs == mine, triangle, bias1)
                bias2 = jnp.where(theirs == mine, triangle, bias2)
            second = slice(GROUP * RUN, Q_ROWS)
            fold(qb[c, :Q_ROWS, :], k1, v1, bias1, m.at[c], l.at[c], a.at[c], first)
            fold(qb[c, second, :], k2, v2, bias2, m.at[c, second], l.at[c, second], a.at[c, second], False)

    eye = lax.broadcasted_iota(jnp.int32, (HD, HD), 0) == lax.broadcasted_iota(jnp.int32, (HD, HD), 1)

    def close(c, dst):
        total = jnp.sum(l[c], axis=1, keepdims=True)
        dst[:Q_ROWS, :] = (a[c] * (1.0 / total)).astype(BF16)
        logs = m[c] * SCALE + jnp.log2(total)
        rows = []
        for g in range(GROUP):
            starts = [(r * GROUP + g) * RUN for r in range(2)]
            both = jnp.concatenate([logs[i : i + RUN] for i in starts], axis=0)
            rows.append(jnp.sum(jnp.where(eye, both, 0.0), axis=0, keepdims=True))
        rest = jnp.concatenate(rows, axis=0)
        pieces = []
        for unused in range(3):
            piece = rest.astype(BF16).astype(F32)
            rest = rest - piece
            pieces.append(piece)
        pieces.append(jnp.zeros_like(rest))
        dst[Q_ROWS:, :] = jnp.concatenate(pieces, axis=0).astype(BF16)

    to_row = lax.broadcasted_iota(jnp.int32, (HD, HD), 0)
    from_row = lax.broadcasted_iota(jnp.int32, (HD, HD), 1)
    place = to_row == jnp.where(swapped > 0.5, lax.bitwise_xor(from_row, RUN), from_row)

    def merge(h, sources):
        logs = []
        for i in sources:
            t = ob[i, Q_ROWS:, :].astype(F32)
            logs.append(t[0:4] + t[4:8] + t[8:12])
        top = functools.reduce(jnp.maximum, logs)
        weights = [jnp.exp2(x - top) for x in logs]
        total = sum(weights[1:], weights[0])
        weights = [w / total for w in weights]
        for g in range(GROUP):
            left, right = [], []
            for w, i in zip(weights, sources):
                spread = jnp.where(place, w[g : g + 1, :], 0.0)
                high = spread.astype(BF16)
                left += [high, (spread - high.astype(F32)).astype(BF16)]
                part = [ob[i, (r * GROUP + g) * RUN : (r * GROUP + g + 1) * RUN, :] for r in range(2)]
                right += part + part
            o = nn(jnp.concatenate(left, axis=1), jnp.concatenate(right, axis=0))
            out_ref[:, columns(h, g, GROUP)] = o.astype(BF16)
        whole = (top + jnp.log2(total)) * math.log(2.0)
        turned = jnp.concatenate([whole[:, RUN:], whole[:, :RUN]], axis=1)
        return jnp.where(swapped > 0.5, turned, whole)

    own = kv.at[SLOT["OO", 0]]
    loads[0].wait()
    loads[1].wait()
    stage_kv(head, own)
    stage_kv(1 - head, spare)
    loads[2].wait()
    stage_q(1 - head, qspare)
    stage_q(head, qb.at[0])
    pl.semaphore_wait(barrier, len(greet))
    send_kv(own, ("ZO", 0), across)
    send_kv(spare, ("ZX", 0), diagonal)
    send_kv(own, ("OO", -1), up)
    send_kv(own, ("OO", 1), down)
    send_kv(spare, ("OX", 0), beside)
    send_kv(spare, ("OX", -1), above)
    send_kv(spare, ("OX", 1), below)
    for i in (3, 1, 2):
        q_copy(i).start()
    for what, *rest in PLAN:
        if what == "query":
            for i in (1, 2, 3):
                q_copy(i).wait_recv()
        else:
            {"pass": pass_on, "far": far, "wait": wait, "attend": attend}[what](*rest)
    for i in (3, 1, 2, 0):
        for chunk in LAST:
            attend(chunk, (i,))
        if i:
            close(i, osend.at[i])
            o_copy(i).start()
        else:
            close(0, ob.at[0])
    o_copy(3).wait_recv()
    mine = merge(head, (0, 3))
    o_copy(1).wait_recv()
    o_copy(2).wait_recv()
    other = merge(1 - head, (1, 2))
    even = jnp.where(head == 0, 1.0, 0.0)
    lse_ref[0:GROUP, :] = jnp.where(even > 0.5, mine, other)
    lse_ref[GROUP:, :] = jnp.where(even > 0.5, other, mine)
    for copy in started:
        copy.wait_send()
    for i in (1, 2, 3):
        q_copy(i).wait_send()
        o_copy(i).wait_send()


def shards(queries, keys, values, positions):
    vmem = pl.BlockSpec(memory_space=pltpu.VMEM)
    hbm = pl.BlockSpec(memory_space=pltpu.HBM)
    state = pltpu.VMEM((NX, Q_ROWS, HD), F32)
    shared = pltpu.VMEM((NX, Q_ROWS + META, HD), BF16)
    partial = pltpu.VMEM((NX, Q_ROWS + TAIL, HD), BF16)
    blocks = len(SLOT)
    inputs = (positions.reshape(1, TOK), queries, keys, values)
    return pl.pallas_call(
        kernel,
        name="ring_attention",
        out_shape=(
            jax.ShapeDtypeStruct((TOK, QH * HD), BF16),
            jax.ShapeDtypeStruct((QH, TOK), F32),
        ),
        in_specs=[hbm, hbm, hbm, hbm],
        out_specs=(vmem, vmem),
        scratch_shapes=[
            pltpu.VMEM((1, TOK), jnp.int32),
            pltpu.VMEM((TOK, QH * HD), BF16),
            pltpu.VMEM((TOK, KVH * HD), BF16),
            pltpu.VMEM((TOK, KVH * HD), BF16),
            pltpu.VMEM((blocks, KV_ROWS + META, HD), BF16),
            pltpu.VMEM((KV_ROWS + META, HD), BF16),
            shared,
            pltpu.VMEM((Q_ROWS + META, HD), BF16),
            partial,
            partial,
            state,
            state,
            state,
            pltpu.SemaphoreType.DMA((4,)),
            pltpu.SemaphoreType.DMA((blocks,)),
            pltpu.SemaphoreType.DMA((blocks,)),
            pltpu.SemaphoreType.DMA((NX,)),
            pltpu.SemaphoreType.DMA((NX,)),
            pltpu.SemaphoreType.DMA((NX,)),
            pltpu.SemaphoreType.DMA((NX,)),
        ],
        compiler_params=pltpu.CompilerParams(
            collective_id=0, has_side_effects=True, vmem_limit_bytes=40 * 2**20
        ),
    )(*(pltpu.with_memory_space_constraint(x, pltpu.HBM) for x in inputs))


def solution(mesh):
    return jax.shard_map(
        shards,
        mesh=mesh,
        in_specs=(
            P(("dp", "ctx"), None),
            P(("dp", "ctx"), None),
            P(("dp", "ctx"), None),
            P(("dp", "ctx")),
        ),
        out_specs=(P(("dp", "ctx"), None), P(None, ("dp", "ctx"))),
        check_vma=False,
    )
```
